128 devices in a mesh: frame: 8 (over x, core), row: 16 (over y, z).
Axes of the slice: x: 4, y: 4, z: 4, core: 2. Of those that a mesh axis runs over, the one named last changes fastest.
Arguments:
- video: bfloat16 [128, 32, 32, 512], P(('frame', 'row')), may hold values from -6 to 6
- w_spatial: bfloat16 [3, 3, 512, 512], replicated, may hold values from -0.09375 to 0.09375
- temporal_weight: bfloat16 [3, 512, 512], replicated, may hold values from -0.15625 to 0.15625
- clip_frame_counts: int32 [16], replicated, may hold values from 1 to 24, 128 in all
- cotangent: bfloat16 [128, 32, 32, 512], P(('frame', 'row')), may hold values from -6 to 6
Outputs:
- output: bfloat16 [128, 32, 32, 512], P(('frame', 'row'))
- grad_video: bfloat16 [128, 32, 32, 512], P(('frame', 'row'))
- grad_spatial: float32 [3, 3, 512, 512], replicated
- grad_temporal: float32 [3, 512, 512], replicated
The draws below stay inside these ranges and needn't reach their ends.
Inputs may be any that keep to these rules, and one draw needn't show every extreme that they name: `clip_frame_counts`: clip lengths sum to 128; the longest is exactly 24.
All inputs are finite; a program needn't handle non-finite values.
Results may differ from the reference program's by a relative error of at most 0.0053.
Values may be sent and summed in bfloat16 or wider, within the bound.
A program may use at most 128 MiB of HBM per device.

```python
import math
import jax
import jax.numpy as jnp
import numpy as np
from jax import lax

C = 512
H = 32
W = 32
TIME_DILATION = 2
FRAMES = 128
NCLIPS = 16
LONGEST = 24


def steps_of(stream_key, extent, split, least, top_value):
    def one(axis_at, shards_of):
        heights = jax.random.uniform(jax.random.fold_in(jax.random.fold_in(stream_key, 6), axis_at), (shards_of,), jnp.float32, least / len(split), top_value / len(split))
        return jnp.repeat(jnp.exp(heights), extent[axis_at] // shards_of).reshape((-1,) + (1,) * (len(extent) - axis_at - 1))

    gain = one(*split[0])
    for cut in split[1:]:
        gain = gain * one(*cut)
    return gain


def split_up(number_of, total, bound, slope):
    loads = [(1 << 20) // math.isqrt(standing ** slope) + 1 for standing in range(2, number_of + 1)]
    surplus, holding = total - bound - (number_of - 1), [1] * (number_of - 1)
    while surplus > 0:
        free = [i for i in range(number_of - 1) if holding[i] < bound]
        pool, left = sum([loads[i] for i in free]), surplus
        for i in free:
            extra = min(bound - holding[i], max(1, left * loads[i] // pool), surplus)
            holding[i] = holding[i] + extra
            surplus = surplus - extra
    return np.array([bound] + holding)


def ragged_sizes(key, count, total, bound, slope):
    if count == 2:
        one = jax.random.randint(key, (), max(1, total - bound), min(bound, total - 1) + 1)
        return jnp.stack([one, total - one])
    tallies = jnp.asarray(split_up(count, total, bound, slope), jnp.int32)
    couples = (count - 1) // 2
    source_of, receiver = tallies[1:1 + 2 * couples:2], tallies[2:2 + 2 * couples:2]
    slack = jnp.minimum(source_of - 1, bound - receiver)
    passed = jax.random.randint(jax.random.fold_in(key, 1), (couples,), 0, 1 << 20) % (slack + 1)
    tallies = tallies.at[1:1 + 2 * couples:2].set(source_of - passed).at[2:2 + 2 * couples:2].set(receiver + passed)
    return tallies[jax.random.permutation(jax.random.fold_in(key, 2), count)]


def bell_draw(key, shape, deviation, bound, cuts=(), held_as=jnp.bfloat16):
    values = deviation * jax.random.normal(key, shape, jnp.float32)
    if cuts:
        values = values * steps_of(key, shape, cuts, -0.22, 0.18)
    return jnp.clip(values, -bound, bound).astype(held_as)


def setup_inputs(seed: int = 0) -> dict:
    key_of = jax.random.split(jax.random.key(seed), 6)
    return {
        "video": bell_draw(key_of[0], (FRAMES, H, W, C), 1.0, 6.0, ((0, 128),)),
        "w_spatial": bell_draw(key_of[1], (3, 3, C, C), (9 * C) ** -0.5, 0.09375),
        "temporal_weight": bell_draw(key_of[2], (3, C, C), (3 * C) ** -0.5, 0.15625),
        "clip_frame_counts": ragged_sizes(key_of[3], NCLIPS, FRAMES, LONGEST, 2).astype(jnp.int32),
        "cotangent": bell_draw(key_of[4], (FRAMES, H, W, C), 1.0, 6.0, ((0, 128),)),
    }


def clip_positions(frame_rows, clip_frame_counts):
    ends = jnp.cumsum(clip_frame_counts)
    starts = ends - clip_frame_counts
    clip_of = jnp.sum((frame_rows[:, None] >= ends[None, :]).astype(jnp.int32), axis=1)
    match = clip_of[:, None] == jnp.arange(clip_frame_counts.shape[0], dtype=jnp.int32)[None, :]
    start_of = jnp.sum(jnp.where(match, starts[None, :], 0), axis=1).astype(jnp.int32)
    return frame_rows - start_of


def spatial_terms(video, w_spatial):
    height, width, channels = video.shape[1], video.shape[2], video.shape[3]
    padded = jnp.pad(video, ((0, 0), (1, 1), (1, 1), (0, 0)))
    result = jnp.zeros((video.shape[0] * height * width, channels), jnp.float32)
    for row_off in range(3):
        for col_off in range(3):
            piece = padded[:, row_off:row_off + height, col_off:col_off + width, :].reshape(-1, channels)
            result = result + jnp.dot(piece, w_spatial[row_off, col_off], preferred_element_type=jnp.float32)
    return result


def spatial_back(video, dpre, w_spatial):
    height, width, channels = video.shape[1], video.shape[2], video.shape[3]
    padded = jnp.pad(video, ((0, 0), (1, 1), (1, 1), (0, 0)))
    dpre_grid = dpre.reshape(video.shape)
    dpre_pad = jnp.pad(dpre_grid, ((0, 0), (1, 1), (1, 1), (0, 0)))
    grads = []
    spread = jnp.zeros((video.shape[0] * height * width, channels), jnp.float32)
    for row_off in range(3):
        line = []
        for col_off in range(3):
            piece = padded[:, row_off:row_off + height, col_off:col_off + width, :].reshape(-1, channels)
            line.append(lax.dot_general(piece, dpre, (((0,), (0,)), ((), ())), preferred_element_type=jnp.float32))
            moved = dpre_pad[:, 2 - row_off:2 - row_off + height, 2 - col_off:2 - col_off + width, :].reshape(-1, channels)
            spread = spread + lax.dot_general(moved, w_spatial[row_off, col_off], (((1,), (1,)), ((), ())), preferred_element_type=jnp.float32)
        grads.append(jnp.stack(line))
    return jnp.stack(grads), spread


def temporal_mixing(source_activation, offset, source_cotangent, own_cot, frame_rows, every_frame_rows, clip_frame_counts, temporal_weight):
    count, pixels, channels = own_cot.shape
    place = clip_positions(frame_rows, clip_frame_counts)
    mixed_output = jnp.zeros((count * pixels, channels), jnp.float32)
    activation_gradient = jnp.zeros((count * pixels, channels), jnp.float32)
    grads = []
    for kernel_tap_index in range(3):
        causal_reach = kernel_tap_index * TIME_DILATION
        keep_mask = (place >= causal_reach).astype(jnp.bfloat16)[:, None, None]
        looked = lax.slice_in_dim(source_activation, offset - causal_reach, offset - causal_reach + count, axis=0) * keep_mask
        looked_rows = looked.reshape(-1, channels)
        mixed_output = mixed_output + jnp.dot(looked_rows, temporal_weight[kernel_tap_index], preferred_element_type=jnp.float32)
        grads.append(lax.dot_general(looked_rows, own_cot.reshape(-1, channels), (((0,), (0,)), ((), ())), preferred_element_type=jnp.float32))
        ahead = frame_rows + causal_reach
        ahead_keep = ((clip_positions(ahead, clip_frame_counts) >= causal_reach) & (ahead < every_frame_rows)).astype(jnp.bfloat16)
        ahead_rows = lax.slice_in_dim(source_cotangent, causal_reach, causal_reach + count, axis=0) * ahead_keep[:, None, None]
        activation_gradient = activation_gradient + lax.dot_general(ahead_rows.reshape(-1, channels), temporal_weight[kernel_tap_index], (((1,), (1,)), ((), ())), preferred_element_type=jnp.float32)
    return mixed_output.reshape(count, pixels, channels), activation_gradient.reshape(count, pixels, channels), jnp.stack(grads)


def reference(video, w_spatial, temporal_weight, clip_frame_counts, cotangent):
    every_frame_rows, height, width, channels = video.shape
    pre = spatial_terms(video, w_spatial)
    activation_rows = jax.nn.silu(pre).astype(jnp.bfloat16).reshape(every_frame_rows, height * width, channels)
    output_cotangent = cotangent.reshape(every_frame_rows, height * width, channels)
    frame_rows = jnp.arange(every_frame_rows, dtype=jnp.int32)
    source_activation = jnp.pad(activation_rows, ((2 * TIME_DILATION, 0), (0, 0), (0, 0)))
    source_cotangent = jnp.pad(output_cotangent, ((0, 2 * TIME_DILATION), (0, 0), (0, 0)))
    mixed_output, activation_gradient, temporal_weight_gradient = temporal_mixing(source_activation, 2 * TIME_DILATION, source_cotangent, output_cotangent, frame_rows, every_frame_rows, clip_frame_counts, temporal_weight)
    mixed_b = mixed_output.astype(jnp.bfloat16).reshape(video.shape)
    output = (video.astype(jnp.float32) + mixed_b.astype(jnp.float32)).astype(jnp.bfloat16)
    dact_b = activation_gradient.astype(jnp.bfloat16).reshape(-1, channels)
    sigma = jax.nn.sigmoid(pre)
    dpre = (dact_b.astype(jnp.float32) * sigma * (1.0 + pre * (1.0 - sigma))).astype(jnp.bfloat16)
    grad_s, spread = spatial_back(video, dpre, w_spatial)
    grad_video = (cotangent.astype(jnp.float32) + spread.reshape(video.shape)).astype(jnp.bfloat16)
    scale = jnp.float32(1.0 / (float(every_frame_rows * height * width) ** 0.5))
    return output, grad_video, grad_s * scale, temporal_weight_gradient * scale
```

```python
import functools

import jax
import jax.numpy as jnp
from jax import lax
from jax.experimental import pallas as pl
from jax.experimental.pallas import tpu as pltpu
from jax.sharding import PartitionSpec as P

MESH = pl.DeviceIdType.MESH
F32, BF16 = jnp.float32, jnp.bfloat16
DILATION = 2
FRAMES = 128
CLIPS = 16
HW, WID, C = 1024, 32, 512
PAD = HW + 2 * WID
NCOT = 8
CC = HW // NCOT
NFWD = 4
FC = HW // NFWD
TAPS = 12
GROUPS = ((0, "xyz"), (3, "yxz"), (6, "xyz"), (9, "yxz"))
GT = 3


def nn(a, b):
    return jnp.dot(a, b, preferred_element_type=F32)


def nt(a, b):
    return lax.dot_general(a, b, (((1,), (1,)), ((), ())), preferred_element_type=F32)


def tn(a, b):
    return lax.dot_general(a, b, (((0,), (0,)), ((), ())), preferred_element_type=F32)


def at(start, size):
    return pl.ds(pl.multiple_of(start, 16), size)


def kernel(
    video, w_hbm, tw_hbm, counts, cot,
    out_hbm, gv_hbm, grads_hbm,
    v, d, cotv, c4, c2, a0, a4, a2, slope, w, tw, tacc,
    part, s0, half, r1, s1, r2, s2, r3, full, outv, gvv,
    load_sem, cy_s, cy_r, cz_s, cz_r, ay_s, ay_r, az_s, az_r,
    s0_s, s0_r, rs_s, rs_r, ag_s, ag_r, co_s, co_r, out_sem,
):
    fr, rw = lax.axis_index("frame"), lax.axis_index("row")
    f = fr * 16 + rw
    me = {"x": fr // 2, "c": fr % 2, "y": rw // 4, "z": rw % 4}

    def dev(**new):
        p = {**me, **new}
        return (p["x"] * 2 + p["c"], p["y"] * 4 + p["z"])

    def frame_dev(step):
        g = (f + step + FRAMES) % FRAMES
        return (g // 16, g % 16)

    ahead4, behind4 = frame_dev(4), frame_dev(-4)
    other = dev(c=1 - me["c"])
    zpair = dev(z=(me["z"] + 2) % 4)
    low = me["z"] < 2

    barrier = pltpu.get_barrier_semaphore()
    partners = [dev(**{a: (me[a] + k) % 4}) for a in "xyz" for k in (1, 2, 3)]
    partners += [other, ahead4, behind4]
    for p in partners:
        pl.semaphore_signal(barrier, inc=1, device_id=p, device_id_type=MESH)

    loads = [
        pltpu.make_async_copy(video, v.at[1, pl.ds(WID, HW)], load_sem.at[0]),
        pltpu.make_async_copy(w_hbm, w, load_sem.at[1]),
        pltpu.make_async_copy(cot, cotv, load_sem.at[2]),
        pltpu.make_async_copy(tw_hbm, tw, load_sem.at[3]),
    ]
    for c in loads:
        c.start()
    pl.semaphore_wait(barrier, len(partners))

    def remote(src, dst, ss, rs, to):
        return pltpu.make_async_remote_copy(
            src_ref=src, dst_ref=dst, send_sem=ss, recv_sem=rs, device_id=to, device_id_type=MESH
        )

    def cot_y(i):
        s = at(i * CC, CC)
        return remote(cot.at[s], c4.at[s], cy_s.at[i], cy_r.at[i], behind4)

    def cot_z(i, src):
        s = at(i * CC, CC)
        return remote(src.at[s], c2.at[s], cz_s.at[i], cz_r.at[i], zpair)

    def start_cot(i, _):
        cot_y(i).start()

        @pl.when(jnp.logical_not(low))
        def _():
            cot_z(i, cot).start()

        return 0

    lax.fori_loop(0, NCOT, start_cot, 0)

    def keep(g, reach):
        end = jnp.int32(0)
        start = jnp.int32(0)
        for n in range(CLIPS):
            end = end + counts[n]
            start = jnp.where(end <= g, end, start)
        ok = jnp.logical_and(g - start >= reach, g < FRAMES)
        return jnp.where(ok, jnp.float32(1.0), jnp.float32(0.0))

    k1, k2 = keep(f, DILATION), keep(f, 2 * DILATION)
    m1, m2 = keep(f + DILATION, DILATION), keep(f + 2 * DILATION, 2 * DILATION)

    for j in range(3):
        v[j, pl.ds(0, WID)] = jnp.zeros((WID, C), BF16)
        v[j, pl.ds(PAD - WID, WID)] = jnp.zeros((WID, C), BF16)
        d[j, pl.ds(0, WID)] = jnp.zeros((WID, C), BF16)
        d[j, pl.ds(PAD - WID, WID)] = jnp.zeros((WID, C), BF16)

    def columns(rows):
        return lax.broadcasted_iota(jnp.int32, (rows, C), 0) % WID

    def right_by_one(a, rows):
        return jnp.where(columns(rows) == 0, 0.0, pltpu.roll(a, 1, 0)).astype(BF16)

    def left_by_one(a, rows):
        return jnp.where(columns(rows) == WID - 1, 0.0, pltpu.roll(a, rows - 1, 0)).astype(BF16)

    loads[0].wait()

    def shift_video(r, _):
        s = at(WID + r * FC, FC)
        a = v[1, s].astype(F32)
        v[0, s] = right_by_one(a, FC)
        v[2, s] = left_by_one(a, FC)
        return 0

    lax.fori_loop(0, NFWD, shift_video, 0)
    loads[1].wait()

    def act_y(r):
        s = at(r * FC, FC)
        return remote(a0.at[s], a4.at[s], ay_s.at[r], ay_r.at[r], ahead4)

    def forward(r, _):
        acc = None
        for i in range(3):
            for j in range(3):
                t = nn(v[j, at(r * FC + i * WID, FC)], w[3 * i + j])
                acc = t if acc is None else acc + t
        s = at(r * FC, FC)
        sig = jax.nn.sigmoid(acc)
        a0[s] = (acc * sig).astype(BF16)
        slope[s] = sig * (1.0 + acc * (1.0 - sig))
        act_y(r).start()
        return 0

    lax.fori_loop(0, NFWD, forward, 0)
    loads[2].wait()
    loads[3].wait()

    mine, theirs = at(me["c"] * 256, 256), at((1 - me["c"]) * 256, 256)

    def core_half(t):
        return remote(part.at[t, :, theirs], s0.at[t], s0_s.at[t], s0_r.at[t], other)

    def emit(t, g):
        g = g.astype(BF16)
        for b in range(4):
            part[t, b] = g[:, b * 128 : (b + 1) * 128]
        core_half(t).start()

    emit(0, tn(a0[...], cotv[...]))

    tacc[...] = jnp.zeros_like(tacc)

    def backward(i, _):
        cot_y(i).wait_recv()

        @pl.when(low)
        def _():
            cot_z(i, c4).start()

        s = at(i * CC, CC)
        cot_z(i, c4).wait_recv()
        da = nt(cotv[s], tw[0]) + m1 * nt(c2[s], tw[1]) + m2 * nt(c4[s], tw[2])
        dp = (da.astype(BF16).astype(F32) * slope[s]).astype(BF16)
        e = at(WID + i * CC, CC)
        d[1, e] = dp
        dp = dp.astype(F32)
        d[0, e] = left_by_one(dp, CC)
        d[2, e] = right_by_one(dp, CC)
        tacc[0] += tn(a0[s], c2[s])
        tacc[1] += tn(a0[s], c4[s])
        return 0

    lax.fori_loop(0, NCOT, backward, 0)

    def act_z(src):
        return remote(src, a2, az_s.at[0], az_r.at[0], zpair)

    @pl.when(low)
    def _():
        act_z(a0).start()

    emit(1, m1 * tacc[0])
    emit(2, m2 * tacc[1])

    def ring(g, stage):
        axis = GROUPS[g][1][stage]
        return axis, me[axis]

    def rs(g, stage, k):
        t0 = GROUPS[g][0]
        axis, q = ring(g, stage)
        to = (q + k) % 4
        if stage == 0:
            src, dst = half.at[pl.ds(t0, GT), to], r1.at[g, k - 1]
        elif stage == 1:
            src, dst = s1.at[g, :, at(to * 64, 64)], r2.at[g, k - 1]
        else:
            src, dst = s2.at[g, :, at(to * 16, 16)], r3.at[g, k - 1]
        return remote(src, dst, rs_s.at[g, stage, k - 1], rs_r.at[g, stage, k - 1], dev(**{axis: to}))

    def rs_start(g, stage):
        for k in (2, 1, 3):
            rs(g, stage, k).start()

    def open_group(g):
        def add(n, _):
            t = GROUPS[g][0] + n
            core_half(t).wait_recv()
            half[t] = (part[t, :, mine].astype(F32) + s0[t].astype(F32)).astype(BF16)
            return 0

        lax.fori_loop(0, GT, add, 0)
        rs_start(g, 0)

    def close_stage(g, stage):
        for k in (1, 3, 2):
            rs(g, stage, k).wait_recv()
        axis, q = ring(g, stage)
        if stage == 0:
            own, got = half[pl.ds(GROUPS[g][0], GT), q], r1
        elif stage == 1:
            own, got = s1[g, :, at(q * 64, 64)], r2
        else:
            own, got = s2[g, :, at(q * 16, 16)], r3
        total = own.astype(F32) + got[g, 0].astype(F32) + got[g, 1].astype(F32) + got[g, 2].astype(F32)
        total = total.astype(BF16)
        if stage == 0:
            s1[g] = total
            rs_start(g, 1)
        elif stage == 1:
            s2[g] = total
            rs_start(g, 2)
        else:
            q1, q2 = ring(g, 0)[1], ring(g, 1)[1]
            full[pl.ds(GROUPS[g][0], GT), q1, at(me["c"] * 256 + q2 * 64 + q * 16, 16)] = total
            ag_start(g, 2)

    def ag(g, stage, k):
        t0 = GROUPS[g][0]
        q1, q2, q3 = (ring(g, n)[1] for n in range(3))
        if stage == 2:
            rows = at(me["c"] * 256 + q2 * 64 + q3 * 16, 16)
        elif stage == 1:
            rows = at(me["c"] * 256 + q2 * 64, 64)
        else:
            rows = at(me["c"] * 256, 256)
        axis, q = ring(g, stage)
        ref = full.at[pl.ds(t0, GT), q1, rows]
        return remote(ref, ref, ag_s.at[g, stage, k - 1], ag_r.at[g, stage, k - 1], dev(**{axis: (q + k) % 4}))

    def ag_start(g, stage):
        for k in (2, 1, 3):
            ag(g, stage, k).start()

    def to_core(g):
        ref = full.at[pl.ds(GROUPS[g][0], GT), :, mine]
        return remote(ref, ref, co_s.at[g], co_r.at[g], other)

    def ag_close(g, stage):
        for k in (1, 3, 2):
            ag(g, stage, k).wait_recv()
        if stage > 0:
            ag_start(g, stage - 1)
        else:
            to_core(g).start()

    def spatial_taps(i):
        def one(j, _):
            emit(3 + 3 * i + j, tn(v[1, pl.ds(WID, HW)], d[j, pl.ds((2 - i) * WID, HW)]))
            return 0

        lax.fori_loop(0, 3, one, 0)

    def grad_video(r, _):
        acc = None
        for i in range(3):
            for j in range(3):
                t = nt(d[j, at(r * FC + (2 - i) * WID, FC)], w[3 * i + j])
                acc = t if acc is None else acc + t
        s = at(r * FC, FC)
        gvv[s] = (cotv[s].astype(F32) + acc).astype(BF16)
        return 0

    def mix(r, _):
        s = at(r * FC, FC)
        t = nn(a0[s], tw[0]) + k1 * nn(a2[s], tw[1]) + k2 * nn(a4[s], tw[2])
        t = t.astype(BF16).astype(F32)
        outv[s] = (v[1, at(WID + r * FC, FC)].astype(F32) + t).astype(BF16)
        return 0

    spatial_taps(0)
    open_group(0)
    spatial_taps(1)
    open_group(1)
    spatial_taps(2)
    open_group(2)

    def wait_act(r, _):
        act_y(r).wait_recv()
        return 0

    lax.fori_loop(0, NFWD, wait_act, 0)

    @pl.when(jnp.logical_not(low))
    def _():
        act_z(a4).start()

    open_group(3)
    lax.fori_loop(0, 2, grad_video, 0)
    close_stage(0, 0)
    lax.fori_loop(2, NFWD, grad_video, 0)
    gv_out = pltpu.make_async_copy(gvv, gv_hbm, out_sem.at[0])
    gv_out.start()
    close_stage(1, 0)
    close_stage(0, 1)
    close_stage(1, 1)
    close_stage(0, 2)
    close_stage(1, 2)
    close_stage(2, 0)
    close_stage(3, 0)
    ag_close(0, 2)
    ag_close(1, 2)
    close_stage(2, 1)
    close_stage(3, 1)
    ag_close(0, 1)
    ag_close(1, 1)
    close_stage(2, 2)
    close_stage(3, 2)
    ag_close(2, 2)
    ag_close(3, 2)
    ag_close(2, 1)
    ag_close(3, 1)
    act_z(a0).wait_recv()
    lax.fori_loop(0, NFWD, mix, 0)
    out_out = pltpu.make_async_copy(outv, out_hbm, out_sem.at[1])
    out_out.start()

    def grads_out(g, rows, n):
        taps = pl.ds(GROUPS[g][0], GT)
        return pltpu.make_async_copy(full.at[taps, :, rows], grads_hbm.at[taps, :, rows], out_sem.at[2 + 2 * g + n])

    for g in range(len(GROUPS)):
        ag_close(g, 0)
        grads_out(g, mine, 0).start()
    for g in range(len(GROUPS)):
        to_core(g).wait_recv()
        grads_out(g, theirs, 1).start()

    def drain_cot(i, _):
        cot_y(i).wait_send()
        cot_z(i, c4).wait_send()
        return 0

    lax.fori_loop(0, NCOT, drain_cot, 0)

    def drain_act(r, _):
        act_y(r).wait_send()
        return 0

    lax.fori_loop(0, NFWD, drain_act, 0)
    act_z(a0).wait_send()

    def drain_core(t, _):
        core_half(t).wait_send()
        return 0

    lax.fori_loop(0, TAPS, drain_core, 0)
    for g in range(len(GROUPS)):
        for stage in range(3):
            for k in (1, 2, 3):
                rs(g, stage, k).wait_send()
                ag(g, stage, k).wait_send()
        to_core(g).wait_send()
    gv_out.wait()
    out_out.wait()
    for g in range(len(GROUPS)):
        grads_out(g, mine, 0).wait()
        grads_out(g, theirs, 1).wait()


def on_device(video, w_spatial, temporal_weight, clip_frame_counts, cotangent):
    n = len(GROUPS)
    dma = pltpu.SemaphoreType.DMA
    any_spec = pl.BlockSpec(memory_space=pl.ANY)
    frame = (HW, C)
    out, gv, grads = pl.pallas_call(
        kernel,
        out_shape=(
            jax.ShapeDtypeStruct(frame, BF16),
            jax.ShapeDtypeStruct(frame, BF16),
            jax.ShapeDtypeStruct((TAPS, 4, C, 128), BF16),
        ),
        in_specs=[any_spec, any_spec, any_spec, pl.BlockSpec(memory_space=pltpu.SMEM), any_spec],
        out_specs=(any_spec, any_spec, any_spec),
        scratch_shapes=[
            pltpu.VMEM((3, PAD, C), BF16),
            pltpu.VMEM((3, PAD, C), BF16),
            pltpu.VMEM(frame, BF16),
            pltpu.VMEM(frame, BF16),
            pltpu.VMEM(frame, BF16),
            pltpu.VMEM(frame, BF16),
            pltpu.VMEM(frame, BF16),
            pltpu.VMEM(frame, BF16),
            pltpu.VMEM(frame, F32),
            pltpu.VMEM((9, C, C), BF16),
            pltpu.VMEM((3, C, C), BF16),
            pltpu.VMEM((2, C, C), F32),
            pltpu.VMEM((TAPS, 4, C, 128), BF16),
            pltpu.VMEM((TAPS, 4, 256, 128), BF16),
            pltpu.VMEM((TAPS, 4, 256, 128), BF16),
            pltpu.VMEM((n, 3, GT, 256, 128), BF16),
            pltpu.VMEM((n, GT, 256, 128), BF16),
            pltpu.VMEM((n, 3, GT, 64, 128), BF16),
            pltpu.VMEM((n, GT, 64, 128), BF16),
            pltpu.VMEM((n, 3, GT, 16, 128), BF16),
            pltpu.VMEM((TAPS, 4, C, 128), BF16),
            pltpu.VMEM(frame, BF16),
            pltpu.VMEM(frame, BF16),
            dma((4,)),
            dma((NCOT,)), dma((NCOT,)), dma((NCOT,)), dma((NCOT,)),
            dma((NFWD,)), dma((NFWD,)), dma((1,)), dma((1,)),
            dma((TAPS,)), dma((TAPS,)),
            dma((n, 3, 3)), dma((n, 3, 3)), dma((n, 3, 3)), dma((n, 3, 3)),
            dma((n,)), dma((n,)),
            dma((2 + 2 * n,)),
        ],
        compiler_params=pltpu.CompilerParams(
            collective_id=0, has_side_effects=True, vmem_limit_bytes=62 << 20
        ),
        name="block",
    )(
        video.reshape(frame),
        w_spatial.reshape(9, C, C),
        temporal_weight,
        clip_frame_counts,
        cotangent.reshape(frame),
    )
    scale = jnp.float32(1.0 / float(FRAMES * HW) ** 0.5)
    grads = grads.transpose(0, 2, 1, 3).reshape(TAPS, C, C).astype(F32) * scale
    return (
        out.reshape(video.shape),
        gv.reshape(video.shape),
        grads[3:].reshape(3, 3, C, C),
        grads[:3],
    )


def solution(mesh):
    frames = P(("frame", "row"), None, None, None)
    return jax.shard_map(
        on_device,
        mesh=mesh,
        in_specs=(frames, P(), P(), P(), frames),
        out_specs=(frames, frames, P(), P()),
        check_vma=False,
    )
```

```python
import functools

import jax
import jax.numpy as jnp
from jax import lax
from jax.experimental import pallas as pl
from jax.experimental.pallas import tpu as pltpu
from jax.sharding import PartitionSpec as P

MESH = pl.DeviceIdType.MESH
F32, BF16 = jnp.float32, jnp.bfloat16
DILATION = 2
FRAMES = 128
CLIPS = 16
HW, WID, C = 1024, 32, 512
PAD = HW + 2 * WID
NCOT = 8
CC = HW // NCOT
EARLY = 3
NFWD = 4
FC = HW // NFWD
TAPS = 12
GROUPS = (
    (0, 1, "xyz"),
    (1, 2, "xyz"),
    (3, 2, "yxz"),
    (5, 2, "xyz"),
    (7, 2, "yxz"),
    (9, 1, "zxy"),
    (10, 2, "xyz"),
)
NG = len(GROUPS)
OPENED = (0, 33, 34, 36, 38, 39, 40)
AFTER = (6, 10, 13, 15, 18, 26)
MIX_AT = 57


def nn(a, b):
    return jnp.dot(a, b, preferred_element_type=F32)


def nt(a, b):
    return lax.dot_general(a, b, (((1,), (1,)), ((), ())), preferred_element_type=F32)


def tn(a, b):
    return lax.dot_general(a, b, (((0,), (0,)), ((), ())), preferred_element_type=F32)


def at(start, size):
    return pl.ds(pl.multiple_of(start, 16), size)


def kernel(
    video, w_hbm, tw_hbm, counts, cot,
    outv, gvv, full,
    v, d, cotv, c4, c2, a0, a4, a2, slope, w, tw, tacc,
    part, s0, half, r1, s1, r2, s2, r3,
    load_sem, cy_s, cy_r, cz_s, cz_r, ay_s, ay_r, az_s, az_r,
    s0_s, s0_r, rs_s, rs_r, ag_s, ag_r, co_s, co_r,
):
    fr, rw = lax.axis_index("frame"), lax.axis_index("row")
    f = fr * 16 + rw
    me = {"x": fr // 2, "c": fr % 2, "y": rw // 4, "z": rw % 4}

    def dev(**new):
        p = {**me, **new}
        return (p["x"] * 2 + p["c"], p["y"] * 4 + p["z"])

    def frame_dev(step):
        g = (f + step + FRAMES) % FRAMES
        return (g // 16, g % 16)

    ahead4, behind4 = frame_dev(4), frame_dev(-4)
    other = dev(c=1 - me["c"])
    zpair = dev(z=(me["z"] + 2) % 4)
    low = me["z"] < 2

    barrier = pltpu.get_barrier_semaphore()
    partners = [dev(**{a: (me[a] + k) % 4}) for a in "xyz" for k in (1, 2, 3)]
    partners += [other, ahead4, behind4]
    for p in partners:
        pl.semaphore_signal(barrier, inc=1, device_id=p, device_id_type=MESH)

    loads = [
        pltpu.make_async_copy(video, v.at[1, pl.ds(WID, HW)], load_sem.at[0]),
        pltpu.make_async_copy(w_hbm, w, load_sem.at[1]),
        pltpu.make_async_copy(cot, cotv, load_sem.at[2]),
        pltpu.make_async_copy(tw_hbm, tw, load_sem.at[3]),
    ]
    for c in loads:
        c.start()
    pl.semaphore_wait(barrier, len(partners))

    def remote(src, dst, ss, rs, to):
        return pltpu.make_async_remote_copy(
            src_ref=src, dst_ref=dst, send_sem=ss, recv_sem=rs, device_id=to, device_id_type=MESH
        )

    def cot_y(i):
        s = at(i * CC, CC)
        return remote(cot.at[s], c4.at[s], cy_s.at[i], cy_r.at[i], behind4)

    def cot_z(i, src):
        s = at(i * CC, CC)
        return remote(src.at[s], c2.at[s], cz_s.at[i], cz_r.at[i], zpair)

    def start_cot(i, _):
        cot_y(i).start()

        @pl.when(jnp.logical_not(low))
        def _():
            cot_z(i, cot).start()

        return 0

    lax.fori_loop(0, NCOT, start_cot, 0)

    def keep(g, reach):
        end = jnp.int32(0)
        start = jnp.int32(0)
        for n in range(CLIPS):
            end = end + counts[n]
            start = jnp.where(end <= g, end, start)
        ok = jnp.logical_and(g - start >= reach, g < FRAMES)
        return jnp.where(ok, jnp.float32(1.0), jnp.float32(0.0))

    k1, k2 = keep(f, DILATION), keep(f, 2 * DILATION)
    m1, m2 = keep(f + DILATION, DILATION), keep(f + 2 * DILATION, 2 * DILATION)

    for j in range(3):
        v[j, pl.ds(0, WID)] = jnp.zeros((WID, C), BF16)
        v[j, pl.ds(PAD - WID, WID)] = jnp.zeros((WID, C), BF16)
        d[j, pl.ds(0, WID)] = jnp.zeros((WID, C), BF16)
        d[j, pl.ds(PAD - WID, WID)] = jnp.zeros((WID, C), BF16)

    def columns(rows):
        return lax.broadcasted_iota(jnp.int32, (rows, C), 0) % WID

    def right_by_one(a, rows):
        return jnp.where(columns(rows) == 0, 0.0, pltpu.roll(a, 1, 0)).astype(BF16)

    def left_by_one(a, rows):
        return jnp.where(columns(rows) == WID - 1, 0.0, pltpu.roll(a, rows - 1, 0)).astype(BF16)

    loads[0].wait()

    def shift_video(r, _):
        s = at(WID + r * FC, FC)
        a = v[1, s].astype(F32)
        v[0, s] = right_by_one(a, FC)
        v[2, s] = left_by_one(a, FC)
        return 0

    lax.fori_loop(0, NFWD, shift_video, 0)
    loads[1].wait()

    def act_y(r):
        s = at(r * FC, FC)
        return remote(a0.at[s], a4.at[s], ay_s.at[r], ay_r.at[r], ahead4)

    def forward(r, _):
        acc = None
        for i in range(3):
            for j in range(3):
                t = nn(v[j, at(r * FC + i * WID, FC)], w[3 * i + j])
                acc = t if acc is None else acc + t
        s = at(r * FC, FC)
        sig = jax.nn.sigmoid(acc)
        a0[s] = (acc * sig).astype(BF16)
        slope[s] = sig * (1.0 + acc * (1.0 - sig))
        act_y(r).start()
        return 0

    def forward_cot(i):
        cot_y(i).wait_recv()

        @pl.when(low)
        def _():
            cot_z(i, c4).start()

    lax.fori_loop(0, 2, forward, 0)
    forward_cot(0)
    lax.fori_loop(2, NFWD, forward, 0)
    forward_cot(1)
    loads[2].wait()
    loads[3].wait()

    mine, theirs = at(me["c"] * 256, 256), at((1 - me["c"]) * 256, 256)

    def core_half(t):
        return remote(part.at[t, :, theirs], s0.at[t], s0_s.at[t], s0_r.at[t], other)

    def emit(t, g):
        g = g.astype(BF16)
        for b in range(4):
            part[t, b] = g[:, b * 128 : (b + 1) * 128]
        core_half(t).start()

    emit(0, tn(a0[...], cotv[...]))
    forward_cot(2)

    def ring(g, stage):
        axis = GROUPS[g][2][stage]
        return axis, me[axis]

    def group_taps(g):
        return pl.ds(GROUPS[g][0], GROUPS[g][1])

    def rs(g, stage, k):
        taps = group_taps(g)
        axis, q = ring(g, stage)
        to = (q + k) % 4
        if stage == 0:
            src, dst = half.at[taps, to], r1.at[k - 1, taps]
        elif stage == 1:
            src, dst = s1.at[taps, at(to * 64, 64)], r2.at[k - 1, taps]
        else:
            src, dst = s2.at[taps, at(to * 16, 16)], r3.at[k - 1, taps]
        return remote(src, dst, rs_s.at[g, stage, k - 1], rs_r.at[g, stage, k - 1], dev(**{axis: to}))

    def rs_start(g, stage):
        for k in (2, 1, 3):
            rs(g, stage, k).start()

    def open_group(g):
        def add(n, _):
            t = GROUPS[g][0] + n
            core_half(t).wait_recv()
            half[t] = (part[t, :, mine].astype(F32) + s0[t].astype(F32)).astype(BF16)
            return 0

        lax.fori_loop(0, GROUPS[g][1], add, 0)
        rs_start(g, 0)

    def close_stage(g, stage):
        for k in (1, 3, 2):
            rs(g, stage, k).wait_recv()
        axis, q = ring(g, stage)
        taps = group_taps(g)
        if stage == 0:
            own, got = half[taps, q], r1
        elif stage == 1:
            own, got = s1[taps, at(q * 64, 64)], r2
        else:
            own, got = s2[taps, at(q * 16, 16)], r3
        total = own.astype(F32)
        for k in range(3):
            total = total + got[k, taps].astype(F32)
        total = total.astype(BF16)
        if stage == 0:
            s1[taps] = total
            rs_start(g, 1)
        elif stage == 1:
            s2[taps] = total
            rs_start(g, 2)
        else:
            q1, q2 = ring(g, 0)[1], ring(g, 1)[1]
            full[taps, q1, at(me["c"] * 256 + q2 * 64 + q * 16, 16)] = total
            ag_start(g, 2)

    def ag(g, stage, k):
        q1, q2, q3 = (ring(g, n)[1] for n in range(3))
        if stage == 2:
            rows = at(me["c"] * 256 + q2 * 64 + q3 * 16, 16)
        elif stage == 1:
            rows = at(me["c"] * 256 + q2 * 64, 64)
        else:
            rows = at(me["c"] * 256, 256)
        axis, q = ring(g, stage)
        ref = full.at[group_taps(g), q1, rows]
        return remote(ref, ref, ag_s.at[g, stage, k - 1], ag_r.at[g, stage, k - 1], dev(**{axis: (q + k) % 4}))

    def ag_start(g, stage):
        for k in (2, 1, 3):
            ag(g, stage, k).start()

    def to_core(g):
        ref = full.at[group_taps(g), :, mine]
        return remote(ref, ref, co_s.at[g], co_r.at[g], other)

    def ag_close(g, stage):
        for k in (1, 3, 2):
            ag(g, stage, k).wait_recv()
        if stage > 0:
            ag_start(g, stage - 1)
        else:
            to_core(g).start()

    tacc[...] = jnp.zeros_like(tacc)

    def backward(i, _):
        @pl.when(i >= EARLY)
        def _():
            forward_cot(i)

        s = at(i * CC, CC)
        cot_z(i, c4).wait_recv()
        da = nt(cotv[s], tw[0]) + m1 * nt(c2[s], tw[1]) + m2 * nt(c4[s], tw[2])
        dp = (da.astype(BF16).astype(F32) * slope[s]).astype(BF16)
        e = at(WID + i * CC, CC)
        d[1, e] = dp
        dp = dp.astype(F32)
        d[0, e] = left_by_one(dp, CC)
        d[2, e] = right_by_one(dp, CC)
        tacc[0] += tn(a0[s], c2[s])
        tacc[1] += tn(a0[s], c4[s])
        return 0

    lax.fori_loop(0, 1, backward, 0)
    open_group(0)
    lax.fori_loop(1, 3, backward, 0)
    close_stage(0, 0)
    lax.fori_loop(3, 4, backward, 0)
    close_stage(0, 1)
    lax.fori_loop(4, 5, backward, 0)
    close_stage(0, 2)
    lax.fori_loop(5, 6, backward, 0)
    ag_close(0, 2)
    lax.fori_loop(6, 7, backward, 0)
    ag_close(0, 1)
    lax.fori_loop(7, NCOT, backward, 0)
    ag_close(0, 0)

    def act_z(src, r):
        s = at(r * FC, FC)
        return remote(src.at[s], a2.at[s], az_s.at[r], az_r.at[r], zpair)

    @pl.when(low)
    def _():
        for r in range(NFWD):
            act_z(a0, r).start()

    emit(1, m1 * tacc[0])
    emit(2, m2 * tacc[1])

    def spatial_tap(t):
        i, j = divmod(t - 3, 3)
        emit(t, tn(v[1, pl.ds(WID, HW)], d[j, pl.ds((2 - i) * WID, HW)]))

    def grad_video(r, _):
        acc = None
        for i in range(3):
            for j in range(3):
                t = nt(d[j, at(r * FC + (2 - i) * WID, FC)], w[3 * i + j])
                acc = t if acc is None else acc + t
        s = at(r * FC, FC)
        gvv[s] = (cotv[s].astype(F32) + acc).astype(BF16)
        return 0

    def mix(r, _):
        s = at(r * FC, FC)
        t = nn(a0[s], tw[0]) + k1 * nn(a2[s], tw[1]) + k2 * nn(a4[s], tw[2])
        t = t.astype(BF16).astype(F32)
        outv[s] = (v[1, at(WID + r * FC, FC)].astype(F32) + t).astype(BF16)
        return 0

    def forward_act(r):
        act_y(r).wait_recv()

        @pl.when(jnp.logical_not(low))
        def _():
            act_z(a4, r).start()

    def act_here(r, _):
        act_z(a0, r).wait_recv()
        return 0

    def mix_all():
        lax.fori_loop(0, NFWD, act_here, 0)
        lax.fori_loop(0, NFWD, mix, 0)

    forward_act(0)
    forward_act(1)
    spatial_tap(3)
    open_group(1)
    forward_act(2)
    spatial_tap(4)
    spatial_tap(5)
    open_group(2)
    spatial_tap(6)
    spatial_tap(7)
    open_group(3)
    spatial_tap(8)
    spatial_tap(9)
    open_group(4)
    forward_act(3)
    spatial_tap(10)
    open_group(5)
    spatial_tap(11)
    lax.fori_loop(0, 1, grad_video, 0)
    open_group(6)

    steps = []
    for g in range(1, NG):
        for n, after in enumerate(AFTER):
            steps.append((OPENED[g] + after, g, n))
    for n in range(1, 4):
        steps.append((38 + 2 * n, 0, 10 + n))
    steps.append((MIX_AT, 0, 20))
    for _, g, n in sorted(steps):
        if n == 20:
            mix_all()
        elif n >= 10:
            lax.fori_loop(n - 10, n - 9, grad_video, 0)
        elif n < 3:
            close_stage(g, n)
        else:
            ag_close(g, 5 - n)
    for g in range(NG):
        to_core(g).wait_recv()

    def drain_cot(i, _):
        cot_y(i).wait_send()
        cot_z(i, c4).wait_send()
        return 0

    lax.fori_loop(0, NCOT, drain_cot, 0)

    def drain_act(r, _):
        act_y(r).wait_send()
        act_z(a0, r).wait_send()
        return 0

    lax.fori_loop(0, NFWD, drain_act, 0)

    def drain_core(t, _):
        core_half(t).wait_send()
        return 0

    lax.fori_loop(0, TAPS, drain_core, 0)
    for g in range(NG):
        for stage in range(3):
            for k in (1, 2, 3):
                rs(g, stage, k).wait_send()
                ag(g, stage, k).wait_send()
        to_core(g).wait_send()

def finish(scale, grads, out_in, gv_in, spatial, temporal, out, gv):
    t = pl.program_id(0)
    s = at(jnp.minimum(t, 7) * (HW // 8), HW // 8)
    out[...] = out_in[s]
    gv[...] = gv_in[s]

    def write(ref):
        for b in range(4):
            ref[0, :, b * 128 : (b + 1) * 128] = grads[t, b].astype(F32) * scale

    @pl.when(t < 3)
    def _():
        write(temporal)

    @pl.when(t >= 3)
    def _():
        write(spatial)


def on_device(video, w_spatial, temporal_weight, clip_frame_counts, cotangent):
    dma = pltpu.SemaphoreType.DMA
    any_spec = pl.BlockSpec(memory_space=pl.ANY)
    vmem_spec = pl.BlockSpec(memory_space=pltpu.VMEM)
    frame = (HW, C)
    out, gv, grads = pl.pallas_call(
        kernel,
        out_shape=(
            pltpu.VMEM(frame, BF16),
            pltpu.VMEM(frame, BF16),
            pltpu.VMEM((TAPS, 4, C, 128), BF16),
        ),
        in_specs=[any_spec, any_spec, any_spec, pl.BlockSpec(memory_space=pltpu.SMEM), any_spec],
        out_specs=(vmem_spec, vmem_spec, vmem_spec),
        scratch_shapes=[
            pltpu.VMEM((3, PAD, C), BF16),
            pltpu.VMEM((3, PAD, C), BF16),
            pltpu.VMEM(frame, BF16),
            pltpu.VMEM(frame, BF16),
            pltpu.VMEM(frame, BF16),
            pltpu.VMEM(frame, BF16),
            pltpu.VMEM(frame, BF16),
            pltpu.VMEM(frame, BF16),
            pltpu.VMEM(frame, F32),
            pltpu.VMEM((9, C, C), BF16),
            pltpu.VMEM((3, C, C), BF16),
            pltpu.VMEM((2, C, C), F32),
            pltpu.VMEM((TAPS, 4, C, 128), BF16),
            pltpu.VMEM((TAPS, 4, 256, 128), BF16),
            pltpu.VMEM((TAPS, 4, 256, 128), BF16),
            pltpu.VMEM((3, TAPS, 256, 128), BF16),
            pltpu.VMEM((TAPS, 256, 128), BF16),
            pltpu.VMEM((3, TAPS, 64, 128), BF16),
            pltpu.VMEM((TAPS, 64, 128), BF16),
            pltpu.VMEM((3, TAPS, 16, 128), BF16),
            dma((4,)),
            dma((NCOT,)), dma((NCOT,)), dma((NCOT,)), dma((NCOT,)),
            dma((NFWD,)), dma((NFWD,)), dma((NFWD,)), dma((NFWD,)),
            dma((TAPS,)), dma((TAPS,)),
            dma((NG, 3, 3)), dma((NG, 3, 3)), dma((NG, 3, 3)), dma((NG, 3, 3)),
            dma((NG,)), dma((NG,)),
        ],
        compiler_params=pltpu.CompilerParams(
            collective_id=0, has_side_effects=True, vmem_limit_bytes=54 << 20
        ),
        name="block",
    )(
        video.reshape(frame),
        w_spatial.reshape(9, C, C),
        temporal_weight,
        clip_frame_counts,
        cotangent.reshape(frame),
    )
    scale = 1.0 / float(FRAMES * HW) ** 0.5
    rows = pl.BlockSpec((HW // 8, C), lambda t: (jnp.minimum(t, 7), 0))
    spatial, temporal, out, gv = pl.pallas_call(
        functools.partial(finish, scale),
        grid=(TAPS,),
        out_shape=(
            jax.ShapeDtypeStruct((9, C, C), F32),
            jax.ShapeDtypeStruct((3, C, C), F32),
            jax.ShapeDtypeStruct(frame, BF16),
            jax.ShapeDtypeStruct(frame, BF16),
        ),
        in_specs=[vmem_spec, vmem_spec, vmem_spec],
        out_specs=(
            pl.BlockSpec((1, C, C), lambda t: (jnp.maximum(t - 3, 0), 0, 0)),
            pl.BlockSpec((1, C, C), lambda t: (jnp.minimum(t, 2), 0, 0)),
            rows,
            rows,
        ),
        compiler_params=pltpu.CompilerParams(vmem_limit_bytes=24 << 20),
        name="finish",
    )(*(pltpu.with_memory_space_constraint(a, pltpu.VMEM) for a in (grads, out, gv)))
    return (
        out.reshape(video.shape),
        gv.reshape(video.shape),
        spatial.reshape(3, 3, C, C),
        temporal,
    )


def solution(mesh):
    frames = P(("frame", "row"), None, None, None)
    return jax.shard_map(
        on_device,
        mesh=mesh,
        in_specs=(frames, P(), P(), P(), frames),
        out_specs=(frames, frames, P(), P()),
        check_vma=False,
    )
```

```python
import functools

import jax
import jax.numpy as jnp
from jax import lax
from jax.experimental import pallas as pl
from jax.experimental.pallas import tpu as pltpu
from jax.sharding import PartitionSpec as P

MESH = pl.DeviceIdType.MESH
F32, BF16 = jnp.float32, jnp.bfloat16
DILATION = 2
FRAMES = 128
CLIPS = 16
HW, WID, C = 1024, 32, 512
PAD = HW + 2 * WID
NCOT = 8
CC = HW // NCOT
EARLY = 3
NFWD = 4
FC = HW // NFWD
TAPS = 12
GROUPS = (
    (0, 1, "xyz"),
    (1, 2, "xyz"),
    (3, 2, "yxz"),
    (5, 2, "xyz"),
    (7, 2, "yxz"),
    (9, 1, "zxy"),
    (10, 2, "xyz"),
)
NG = len(GROUPS)
OPENED = (0, 33, 34, 36, 38, 39, 40)
AFTER = (6, 10, 13, 15, 18, 26)
GRAD_VIDEO_AT = (0, 40, 42, 44)
MIX_AT = 57


def nn(a, b):
    return jnp.dot(a, b, preferred_element_type=F32)


def nt(a, b):
    return lax.dot_general(a, b, (((1,), (1,)), ((), ())), preferred_element_type=F32)


def tn(a, b):
    return lax.dot_general(a, b, (((0,), (0,)), ((), ())), preferred_element_type=F32)


def at(start, size):
    return pl.ds(pl.multiple_of(start, 16), size)


def kernel(
    video, w_hbm, tw_hbm, counts, cot,
    outv, gvv, full,
    v, d, cotv, c4, c2, a0, a4, a2, slope, w, tw, tacc,
    part, s0, half, r1, s1, r2, s2, r3,
    load_sem, cy_s, cy_r, cz_s, cz_r, ay_s, ay_r, az_s, az_r,
    s0_s, s0_r, rs_s, rs_r, ag_s, ag_r, co_s, co_r,
):
    fr, rw = lax.axis_index("frame"), lax.axis_index("row")
    f = fr * 16 + rw
    me = {"x": fr // 2, "c": fr % 2, "y": rw // 4, "z": rw % 4}

    def dev(**new):
        p = {**me, **new}
        return (p["x"] * 2 + p["c"], p["y"] * 4 + p["z"])

    def frame_dev(step):
        g = (f + step + FRAMES) % FRAMES
        return (g // 16, g % 16)

    ahead4, behind4 = frame_dev(4), frame_dev(-4)
    other = dev(c=1 - me["c"])
    zpair = dev(z=(me["z"] + 2) % 4)
    low = me["z"] < 2

    barrier = pltpu.get_barrier_semaphore()
    partners = [dev(**{a: (me[a] + k) % 4}) for a in "xyz" for k in (1, 2, 3)]
    partners += [other, ahead4, behind4]
    for p in partners:
        pl.semaphore_signal(barrier, inc=1, device_id=p, device_id_type=MESH)

    loads = [
        pltpu.make_async_copy(video, v.at[1, pl.ds(WID, HW)], load_sem.at[0]),
        pltpu.make_async_copy(w_hbm, w, load_sem.at[1]),
        pltpu.make_async_copy(cot, cotv, load_sem.at[2]),
        pltpu.make_async_copy(tw_hbm, tw, load_sem.at[3]),
    ]
    for c in loads:
        c.start()
    pl.semaphore_wait(barrier, len(partners))

    def remote(src, dst, ss, rs, to):
        return pltpu.make_async_remote_copy(
            src_ref=src, dst_ref=dst, send_sem=ss, recv_sem=rs, device_id=to, device_id_type=MESH
        )

    def cot_y(i):
        s = at(i * CC, CC)
        return remote(cot.at[s], c4.at[s], cy_s.at[i], cy_r.at[i], behind4)

    def cot_z(i, src):
        s = at(i * CC, CC)
        return remote(src.at[s], c2.at[s], cz_s.at[i], cz_r.at[i], zpair)

    def start_cot(i, _):
        cot_y(i).start()

        @pl.when(jnp.logical_not(low))
        def _():
            cot_z(i, cot).start()

        return 0

    lax.fori_loop(0, NCOT, start_cot, 0)

    def keep(g, reach):
        end = jnp.int32(0)
        start = jnp.int32(0)
        for n in range(CLIPS):
            end = end + counts[n]
            start = jnp.where(end <= g, end, start)
        ok = jnp.logical_and(g - start >= reach, g < FRAMES)
        return jnp.where(ok, jnp.float32(1.0), jnp.float32(0.0))

    k1, k2 = keep(f, DILATION), keep(f, 2 * DILATION)
    m1, m2 = keep(f + DILATION, DILATION), keep(f + 2 * DILATION, 2 * DILATION)

    for j in range(3):
        v[j, pl.ds(0, WID)] = jnp.zeros((WID, C), BF16)
        v[j, pl.ds(PAD - WID, WID)] = jnp.zeros((WID, C), BF16)
        d[j, pl.ds(0, WID)] = jnp.zeros((WID, C), BF16)
        d[j, pl.ds(PAD - WID, WID)] = jnp.zeros((WID, C), BF16)

    def columns(rows):
        return lax.broadcasted_iota(jnp.int32, (rows, C), 0) % WID

    def right_by_one(a, rows):
        return jnp.where(columns(rows) == 0, 0.0, pltpu.roll(a, 1, 0)).astype(BF16)

    def left_by_one(a, rows):
        return jnp.where(columns(rows) == WID - 1, 0.0, pltpu.roll(a, rows - 1, 0)).astype(BF16)

    loads[0].wait()

    def shift_video(r, _):
        s = at(WID + r * FC, FC)
        a = v[1, s].astype(F32)
        v[0, s] = right_by_one(a, FC)
        v[2, s] = left_by_one(a, FC)
        return 0

    lax.fori_loop(0, NFWD, shift_video, 0)
    loads[1].wait()

    def act_y(r):
        s = at(r * FC, FC)
        return remote(a0.at[s], a4.at[s], ay_s.at[r], ay_r.at[r], ahead4)

    def forward(r, _):
        acc = None
        for i in range(3):
            for j in range(3):
                t = nn(v[j, at(r * FC + i * WID, FC)], w[3 * i + j])
                acc = t if acc is None else acc + t
        s = at(r * FC, FC)
        sig = jax.nn.sigmoid(acc)
        a0[s] = (acc * sig).astype(BF16)
        slope[s] = sig * (1.0 + acc * (1.0 - sig))
        act_y(r).start()
        return 0

    def forward_cot(i):
        cot_y(i).wait_recv()

        @pl.when(low)
        def _():
            cot_z(i, c4).start()

    lax.fori_loop(0, 2, forward, 0)
    forward_cot(0)
    lax.fori_loop(2, NFWD, forward, 0)
    forward_cot(1)
    loads[2].wait()
    loads[3].wait()

    mine, theirs = at(me["c"] * 256, 256), at((1 - me["c"]) * 256, 256)

    def core_half(t):
        return remote(part.at[t, :, theirs], s0.at[t], s0_s.at[t], s0_r.at[t], other)

    def emit(t, g):
        g = g.astype(BF16)
        for b in range(4):
            part[t, b] = g[:, b * 128 : (b + 1) * 128]
        core_half(t).start()

    emit(0, tn(a0[...], cotv[...]))
    forward_cot(2)

    def ring(g, stage):
        axis = GROUPS[g][2][stage]
        return axis, me[axis]

    def group_taps(g):
        return pl.ds(GROUPS[g][0], GROUPS[g][1])

    def rs(g, stage, k):
        taps = group_taps(g)
        axis, q = ring(g, stage)
        to = (q + k) % 4
        if stage == 0:
            src, dst = half.at[taps, to], r1.at[k - 1, taps]
        elif stage == 1:
            src, dst = s1.at[taps, at(to * 64, 64)], r2.at[k - 1, taps]
        else:
            src, dst = s2.at[taps, at(to * 16, 16)], r3.at[k - 1, taps]
        return remote(src, dst, rs_s.at[g, stage, k - 1], rs_r.at[g, stage, k - 1], dev(**{axis: to}))

    def rs_start(g, stage):
        for k in (2, 1, 3):
            rs(g, stage, k).start()

    def open_group(g):
        def add(n, _):
            t = GROUPS[g][0] + n
            core_half(t).wait_recv()
            half[t] = (part[t, :, mine].astype(F32) + s0[t].astype(F32)).astype(BF16)
            return 0

        lax.fori_loop(0, GROUPS[g][1], add, 0)
        rs_start(g, 0)

    def close_stage(g, stage):
        for k in (1, 3, 2):
            rs(g, stage, k).wait_recv()
        if stage > 0:
            for k in (1, 2, 3):
                rs(g, stage - 1, k).wait_send()
        axis, q = ring(g, stage)
        taps = group_taps(g)
        if stage == 0:
            own, got = half[taps, q], r1
        elif stage == 1:
            own, got = s1[taps, at(q * 64, 64)], r2
        else:
            own, got = s2[taps, at(q * 16, 16)], r3
        total = own.astype(F32)
        for k in range(3):
            total = total + got[k, taps].astype(F32)
        total = total.astype(BF16)
        if stage == 0:
            s1[taps] = total
            rs_start(g, 1)
        elif stage == 1:
            s2[taps] = total
            rs_start(g, 2)
        else:
            q1, q2 = ring(g, 0)[1], ring(g, 1)[1]
            full[taps, q1, at(me["c"] * 256 + q2 * 64 + q * 16, 16)] = total
            ag_start(g, 2)

    def ag(g, stage, k):
        q1, q2, q3 = (ring(g, n)[1] for n in range(3))
        if stage == 2:
            rows = at(me["c"] * 256 + q2 * 64 + q3 * 16, 16)
        elif stage == 1:
            rows = at(me["c"] * 256 + q2 * 64, 64)
        else:
            rows = at(me["c"] * 256, 256)
        axis, q = ring(g, stage)
        ref = full.at[group_taps(g), q1, rows]
        return remote(ref, ref, ag_s.at[g, stage, k - 1], ag_r.at[g, stage, k - 1], dev(**{axis: (q + k) % 4}))

    def ag_start(g, stage):
        for k in (2, 1, 3):
            ag(g, stage, k).start()

    def to_core(g):
        ref = full.at[group_taps(g), :, mine]
        return remote(ref, ref, co_s.at[g], co_r.at[g], other)

    def ag_close(g, stage):
        for k in (1, 3, 2):
            ag(g, stage, k).wait_recv()
        if stage > 0:
            ag_start(g, stage - 1)
        else:
            to_core(g).start()
        for k in (1, 2, 3):
            if stage == 2:
                rs(g, 2, k).wait_send()
            else:
                ag(g, stage + 1, k).wait_send()

    tacc[...] = jnp.zeros_like(tacc)

    def backward(i, _):
        @pl.when(i >= EARLY)
        def _():
            forward_cot(i)

        s = at(i * CC, CC)
        cot_z(i, c4).wait_recv()
        da = nt(cotv[s], tw[0]) + m1 * nt(c2[s], tw[1]) + m2 * nt(c4[s], tw[2])
        dp = (da.astype(BF16).astype(F32) * slope[s]).astype(BF16)
        e = at(WID + i * CC, CC)
        d[1, e] = dp
        dp = dp.astype(F32)
        d[0, e] = left_by_one(dp, CC)
        d[2, e] = right_by_one(dp, CC)
        tacc[0] += tn(a0[s], c2[s])
        tacc[1] += tn(a0[s], c4[s])
        return 0

    lax.fori_loop(0, 1, backward, 0)
    open_group(0)
    lax.fori_loop(1, 3, backward, 0)
    close_stage(0, 0)
    lax.fori_loop(3, 4, backward, 0)
    close_stage(0, 1)
    lax.fori_loop(4, 5, backward, 0)
    close_stage(0, 2)
    lax.fori_loop(5, 6, backward, 0)
    ag_close(0, 2)
    lax.fori_loop(6, 7, backward, 0)
    ag_close(0, 1)
    lax.fori_loop(7, NCOT, backward, 0)
    ag_close(0, 0)

    def act_z(src, r):
        s = at(r * FC, FC)
        return remote(src.at[s], a2.at[s], az_s.at[r], az_r.at[r], zpair)

    emit(1, m1 * tacc[0])
    emit(2, m2 * tacc[1])

    def spatial_tap(t):
        i, j = divmod(t - 3, 3)
        emit(t, tn(v[1, pl.ds(WID, HW)], d[j, pl.ds((2 - i) * WID, HW)]))

    def grad_video(r, _):
        acc = None
        for i in range(3):
            for j in range(3):
                t = nt(d[j, at(r * FC + (2 - i) * WID, FC)], w[3 * i + j])
                acc = t if acc is None else acc + t
        s = at(r * FC, FC)
        gvv[s] = (cotv[s].astype(F32) + acc).astype(BF16)
        return 0

    def mix(r, _):
        s = at(r * FC, FC)
        t = nn(a0[s], tw[0]) + k1 * nn(a2[s], tw[1]) + k2 * nn(a4[s], tw[2])
        t = t.astype(BF16).astype(F32)
        outv[s] = (v[1, at(WID + r * FC, FC)].astype(F32) + t).astype(BF16)
        return 0

    def forward_act(r):
        act_y(r).wait_recv()

        @pl.when(low)
        def _():
            act_z(a0, r).start()

        @pl.when(jnp.logical_not(low))
        def _():
            act_z(a4, r).start()

    def drain_cot(i, _):
        cot_y(i).wait_send()
        cot_z(i, c4).wait_send()
        return 0

    def drain_core(t, _):
        core_half(t).wait_send()
        return 0

    def drain_act(r, _):
        act_y(r).wait_send()
        act_z(a0, r).wait_send()
        return 0

    def act_here(r, _):
        act_z(a0, r).wait_recv()
        return 0

    def mix_all():
        lax.fori_loop(0, NFWD, act_here, 0)
        lax.fori_loop(0, NFWD, mix, 0)
        lax.fori_loop(0, NFWD, drain_act, 0)

    forward_act(0)
    forward_act(1)
    spatial_tap(3)
    open_group(1)
    forward_act(2)
    spatial_tap(4)
    spatial_tap(5)
    open_group(2)
    spatial_tap(6)
    spatial_tap(7)
    open_group(3)
    spatial_tap(8)
    spatial_tap(9)
    open_group(4)
    forward_act(3)
    spatial_tap(10)
    open_group(5)
    spatial_tap(11)
    lax.fori_loop(0, 1, grad_video, 0)
    open_group(6)

    steps = []
    for g in range(1, NG):
        for n, after in enumerate(AFTER):
            steps.append((OPENED[g] + after, g, n))
    for n in range(1, 4):
        steps.append((GRAD_VIDEO_AT[n], 0, 10 + n))
    steps.append((MIX_AT, 0, 20))
    for _, g, n in sorted(steps):
        if n == 20:
            mix_all()
        elif n >= 10:
            lax.fori_loop(n - 10, n - 9, grad_video, 0)
            if n == 11:
                lax.fori_loop(0, NCOT, drain_cot, 0)
            if n == 12:
                lax.fori_loop(0, TAPS, drain_core, 0)
        elif n < 3:
            close_stage(g, n)
        else:
            ag_close(g, 5 - n)
    for g in range(NG):
        to_core(g).wait_recv()
        for k in (1, 2, 3):
            ag(g, 0, k).wait_send()
        to_core(g).wait_send()


def finish(scale, grads, out_in, gv_in, spatial, temporal, out, gv, held, sem):
    copies = [
        pltpu.make_async_copy(out_in, out, sem.at[TAPS]),
        pltpu.make_async_copy(gv_in, gv, sem.at[TAPS + 1]),
    ]
    for c in copies:
        c.start()
    for t in range(TAPS):
        for b in range(4):
            held[t, :, b * 128 : (b + 1) * 128] = grads[t, b].astype(F32) * scale
        to = temporal.at[t] if t < 3 else spatial.at[t - 3]
        copies.append(pltpu.make_async_copy(held.at[t], to, sem.at[t]))
        copies[-1].start()
    for c in copies:
        c.wait()


def on_device(video, w_spatial, temporal_weight, clip_frame_counts, cotangent):
    dma = pltpu.SemaphoreType.DMA
    any_spec = pl.BlockSpec(memory_space=pl.ANY)
    vmem_spec = pl.BlockSpec(memory_space=pltpu.VMEM)
    frame = (HW, C)
    out, gv, grads = pl.pallas_call(
        kernel,
        out_shape=(
            pltpu.VMEM(frame, BF16),
            pltpu.VMEM(frame, BF16),
            pltpu.VMEM((TAPS, 4, C, 128), BF16),
        ),
        in_specs=[any_spec, any_spec, any_spec, pl.BlockSpec(memory_space=pltpu.SMEM), any_spec],
        out_specs=(vmem_spec, vmem_spec, vmem_spec),
        scratch_shapes=[
            pltpu.VMEM((3, PAD, C), BF16),
            pltpu.VMEM((3, PAD, C), BF16),
            pltpu.VMEM(frame, BF16),
            pltpu.VMEM(frame, BF16),
            pltpu.VMEM(frame, BF16),
            pltpu.VMEM(frame, BF16),
            pltpu.VMEM(frame, BF16),
            pltpu.VMEM(frame, BF16),
            pltpu.VMEM(frame, F32),
            pltpu.VMEM((9, C, C), BF16),
            pltpu.VMEM((3, C, C), BF16),
            pltpu.VMEM((2, C, C), F32),
            pltpu.VMEM((TAPS, 4, C, 128), BF16),
            pltpu.VMEM((TAPS, 4, 256, 128), BF16),
            pltpu.VMEM((TAPS, 4, 256, 128), BF16),
            pltpu.VMEM((3, TAPS, 256, 128), BF16),
            pltpu.VMEM((TAPS, 256, 128), BF16),
            pltpu.VMEM((3, TAPS, 64, 128), BF16),
            pltpu.VMEM((TAPS, 64, 128), BF16),
            pltpu.VMEM((3, TAPS, 16, 128), BF16),
            dma((4,)),
            dma((NCOT,)), dma((NCOT,)), dma((NCOT,)), dma((NCOT,)),
            dma((NFWD,)), dma((NFWD,)), dma((NFWD,)), dma((NFWD,)),
            dma((TAPS,)), dma((TAPS,)),
            dma((NG, 3, 3)), dma((NG, 3, 3)), dma((NG, 3, 3)), dma((NG, 3, 3)),
            dma((NG,)), dma((NG,)),
        ],
        compiler_params=pltpu.CompilerParams(
            collective_id=0, has_side_effects=True, vmem_limit_bytes=54 << 20
        ),
        name="block",
    )(
        video.reshape(frame),
        w_spatial.reshape(9, C, C),
        temporal_weight,
        clip_frame_counts,
        cotangent.reshape(frame),
    )
    scale = 1.0 / float(FRAMES * HW) ** 0.5
    spatial, temporal, out, gv = pl.pallas_call(
        functools.partial(finish, scale),
        out_shape=(
            jax.ShapeDtypeStruct((9, C, C), F32),
            jax.ShapeDtypeStruct((3, C, C), F32),
            jax.ShapeDtypeStruct(frame, BF16),
            jax.ShapeDtypeStruct(frame, BF16),
        ),
        in_specs=[vmem_spec, vmem_spec, vmem_spec],
        out_specs=(any_spec, any_spec, any_spec, any_spec),
        scratch_shapes=[pltpu.VMEM((TAPS, C, C), F32), dma((TAPS + 2,))],
        compiler_params=pltpu.CompilerParams(vmem_limit_bytes=24 << 20),
        name="finish",
    )(*(pltpu.with_memory_space_constraint(a, pltpu.VMEM) for a in (grads, out, gv)))
    return (
        out.reshape(video.shape),
        gv.reshape(video.shape),
        spatial.reshape(3, 3, C, C),
        temporal,
    )


def solution(mesh):
    frames = P(("frame", "row"), None, None, None)
    return jax.shard_map(
        on_device,
        mesh=mesh,
        in_specs=(frames, P(), P(), P(), frames),
        out_specs=(frames, frames, P(), P()),
        check_vma=False,
    )
```

```python
import functools

import jax
import jax.numpy as jnp
from jax import lax
from jax.experimental import pallas as pl
from jax.experimental.pallas import tpu as pltpu
from jax.sharding import PartitionSpec as P

MESH = pl.DeviceIdType.MESH
F32, BF16 = jnp.float32, jnp.bfloat16
DILATION = 2
FRAMES = 128
CLIPS = 16
HW, WID, C = 1024, 32, 512
PAD = HW + 2 * WID
NCOT = 8
CC = HW // NCOT
EARLY = 3
NFWD = 4
FC = HW // NFWD
TAPS = 12
GROUPS = (
    (0, 1, "xyz"),
    (1, 2, "xyz"),
    (3, 2, "yxz"),
    (5, 2, "xyz"),
    (7, 2, "yxz"),
    (9, 1, "zxy"),
    (10, 2, "xyz"),
)
NG = len(GROUPS)
OPENED = (0, 33, 34, 36, 38, 39, 40)
AFTER = (6, 10, 13, 15, 18, 24, 28)
GRAD_VIDEO_AT = (0, 40, 42, 44)
MIX_AT = 57


def nn(a, b):
    return jnp.dot(a, b, preferred_element_type=F32)


def nt(a, b):
    return lax.dot_general(a, b, (((1,), (1,)), ((), ())), preferred_element_type=F32)


def tn(a, b):
    return lax.dot_general(a, b, (((0,), (0,)), ((), ())), preferred_element_type=F32)


def at(start, size):
    return pl.ds(pl.multiple_of(start, 16), size)


def kernel(
    video, w_hbm, tw_hbm, counts, cot,
    outv, gvv, full,
    v, d, cotv, c4, c2, a0, a4, a2, slope, w, tw, tacc,
    part, s0, half, r1, s1, r2, s2, r3,
    load_sem, cy_s, cy_r, cz_s, cz_r, ay_s, ay_r, az_s, az_r,
    s0_s, s0_r, rs_s, rs_r, ag_s, ag_r, fw_s, fw_r, co_s, co_r,
):
    fr, rw = lax.axis_index("frame"), lax.axis_index("row")
    f = fr * 16 + rw
    me = {"x": fr // 2, "c": fr % 2, "y": rw // 4, "z": rw % 4}

    def dev(**new):
        p = {**me, **new}
        return (p["x"] * 2 + p["c"], p["y"] * 4 + p["z"])

    def frame_dev(step):
        g = (f + step + FRAMES) % FRAMES
        return (g // 16, g % 16)

    ahead4, behind4 = frame_dev(4), frame_dev(-4)
    other = dev(c=1 - me["c"])
    zpair = dev(z=(me["z"] + 2) % 4)
    low = me["z"] < 2

    barrier = pltpu.get_barrier_semaphore()
    partners = [dev(**{a: (me[a] + k) % 4}) for a in "xyz" for k in (1, 2, 3)]
    partners += [other, ahead4, behind4]
    for p in partners:
        pl.semaphore_signal(barrier, inc=1, device_id=p, device_id_type=MESH)

    loads = [
        pltpu.make_async_copy(video, v.at[1, pl.ds(WID, HW)], load_sem.at[0]),
        pltpu.make_async_copy(w_hbm, w, load_sem.at[1]),
        pltpu.make_async_copy(cot, cotv, load_sem.at[2]),
        pltpu.make_async_copy(tw_hbm, tw, load_sem.at[3]),
    ]
    for c in loads:
        c.start()
    pl.semaphore_wait(barrier, len(partners))

    def remote(src, dst, ss, rs, to):
        return pltpu.make_async_remote_copy(
            src_ref=src, dst_ref=dst, send_sem=ss, recv_sem=rs, device_id=to, device_id_type=MESH
        )

    def cot_y(i):
        s = at(i * CC, CC)
        return remote(cot.at[s], c4.at[s], cy_s.at[i], cy_r.at[i], behind4)

    def cot_z(i, src):
        s = at(i * CC, CC)
        return remote(src.at[s], c2.at[s], cz_s.at[i], cz_r.at[i], zpair)

    def start_cot(i, _):
        cot_y(i).start()

        @pl.when(jnp.logical_not(low))
        def _():
            cot_z(i, cot).start()

        return 0

    lax.fori_loop(0, NCOT, start_cot, 0)

    def keep(g, reach):
        end = jnp.int32(0)
        start = jnp.int32(0)
        for n in range(CLIPS):
            end = end + counts[n]
            start = jnp.where(end <= g, end, start)
        ok = jnp.logical_and(g - start >= reach, g < FRAMES)
        return jnp.where(ok, jnp.float32(1.0), jnp.float32(0.0))

    k1, k2 = keep(f, DILATION), keep(f, 2 * DILATION)
    m1, m2 = keep(f + DILATION, DILATION), keep(f + 2 * DILATION, 2 * DILATION)

    for j in range(3):
        v[j, pl.ds(0, WID)] = jnp.zeros((WID, C), BF16)
        v[j, pl.ds(PAD - WID, WID)] = jnp.zeros((WID, C), BF16)
        d[j, pl.ds(0, WID)] = jnp.zeros((WID, C), BF16)
        d[j, pl.ds(PAD - WID, WID)] = jnp.zeros((WID, C), BF16)

    def columns(rows):
        return lax.broadcasted_iota(jnp.int32, (rows, C), 0) % WID

    def right_by_one(a, rows):
        return jnp.where(columns(rows) == 0, 0.0, pltpu.roll(a, 1, 0)).astype(BF16)

    def left_by_one(a, rows):
        return jnp.where(columns(rows) == WID - 1, 0.0, pltpu.roll(a, rows - 1, 0)).astype(BF16)

    loads[0].wait()

    def shift_video(r, _):
        s = at(WID + r * FC, FC)
        a = v[1, s].astype(F32)
        v[0, s] = right_by_one(a, FC)
        v[2, s] = left_by_one(a, FC)
        return 0

    lax.fori_loop(0, NFWD, shift_video, 0)
    loads[1].wait()

    def act_y(r):
        s = at(r * FC, FC)
        return remote(a0.at[s], a4.at[s], ay_s.at[r], ay_r.at[r], ahead4)

    def forward(r, _):
        acc = None
        for i in range(3):
            for j in range(3):
                t = nn(v[j, at(r * FC + i * WID, FC)], w[3 * i + j])
                acc = t if acc is None else acc + t
        s = at(r * FC, FC)
        sig = jax.nn.sigmoid(acc)
        a0[s] = (acc * sig).astype(BF16)
        slope[s] = sig * (1.0 + acc * (1.0 - sig))
        act_y(r).start()
        return 0

    def forward_cot(i):
        cot_y(i).wait_recv()

        @pl.when(low)
        def _():
            cot_z(i, c4).start()

    lax.fori_loop(0, 2, forward, 0)
    forward_cot(0)
    lax.fori_loop(2, NFWD, forward, 0)
    forward_cot(1)
    loads[2].wait()
    loads[3].wait()

    mine, theirs = at(me["c"] * 256, 256), at((1 - me["c"]) * 256, 256)

    def core_half(t):
        return remote(part.at[t, :, theirs], s0.at[t], s0_s.at[t], s0_r.at[t], other)

    def emit(t, g):
        g = g.astype(BF16)
        for b in range(4):
            part[t, b] = g[:, b * 128 : (b + 1) * 128]
        core_half(t).start()

    emit(0, tn(a0[...], cotv[...]))
    forward_cot(2)

    def ring(g, stage):
        axis = GROUPS[g][2][stage]
        return axis, me[axis]

    def group_taps(g):
        return pl.ds(GROUPS[g][0], GROUPS[g][1])

    def rs(g, stage, k):
        taps = group_taps(g)
        axis, q = ring(g, stage)
        to = (q + k) % 4
        if stage == 0:
            src, dst = half.at[taps, to], r1.at[k - 1, taps]
        elif stage == 1:
            src, dst = s1.at[taps, at(to * 64, 64)], r2.at[k - 1, taps]
        else:
            src, dst = s2.at[taps, at(to * 16, 16)], r3.at[k - 1, taps]
        return remote(src, dst, rs_s.at[g, stage, k - 1], rs_r.at[g, stage, k - 1], dev(**{axis: to}))

    def rs_start(g, stage):
        for k in (2, 1, 3):
            rs(g, stage, k).start()

    def open_group(g):
        def add(n, _):
            t = GROUPS[g][0] + n
            core_half(t).wait_recv()
            half[t] = (part[t, :, mine].astype(F32) + s0[t].astype(F32)).astype(BF16)
            return 0

        lax.fori_loop(0, GROUPS[g][1], add, 0)
        rs_start(g, 0)

    def close_stage(g, stage):
        for k in (1, 3, 2):
            rs(g, stage, k).wait_recv()
        if stage > 0:
            for k in (1, 2, 3):
                rs(g, stage - 1, k).wait_send()
        axis, q = ring(g, stage)
        taps = group_taps(g)
        if stage == 0:
            own, got = half[taps, q], r1
        elif stage == 1:
            own, got = s1[taps, at(q * 64, 64)], r2
        else:
            own, got = s2[taps, at(q * 16, 16)], r3
        total = own.astype(F32)
        for k in range(3):
            total = total + got[k, taps].astype(F32)
        total = total.astype(BF16)
        if stage == 0:
            s1[taps] = total
            rs_start(g, 1)
        elif stage == 1:
            s2[taps] = total
            rs_start(g, 2)
        else:
            q1, q2 = ring(g, 0)[1], ring(g, 1)[1]
            full[taps, q1, at(me["c"] * 256 + q2 * 64 + q * 16, 16)] = total
            ag_start(g, 2)

    def ag(g, stage, k):
        q1, q2, q3 = (ring(g, n)[1] for n in range(3))
        if stage == 2:
            rows = at(me["c"] * 256 + q2 * 64 + q3 * 16, 16)
        elif stage == 1:
            rows = at(me["c"] * 256 + q2 * 64, 64)
        else:
            rows = at(me["c"] * 256, 256)
        axis, q = ring(g, stage)
        ref = full.at[group_taps(g), q1, rows]
        return remote(ref, ref, ag_s.at[g, stage, k - 1], ag_r.at[g, stage, k - 1], dev(**{axis: (q + k) % 4}))

    def ag_start(g, stage):
        for k in (2, 1, 3) if stage > 0 else (1, 3):
            ag(g, stage, k).start()

    def to_core(g):
        ref = full.at[group_taps(g), :, mine]
        return remote(ref, ref, co_s.at[g], co_r.at[g], other)

    def passed(g, way):
        axis, q = ring(g, 0)
        n = 0 if way == 1 else 1
        ref = full.at[group_taps(g), (q + 4 - way) % 4, at(me["c"] * 256 + 128 * n, 128)]
        return remote(ref, ref, fw_s.at[g, n], fw_r.at[g, n], dev(**{axis: (q + 4 + way) % 4}))

    def ag_pass(g):
        ag(g, 0, 1).wait_recv()
        passed(g, 1).start()
        ag(g, 0, 3).wait_recv()
        passed(g, -1).start()
        for k in (1, 2, 3):
            ag(g, 1, k).wait_send()

    def ag_close(g, stage):
        if stage == 0:
            passed(g, 1).wait_recv()
            passed(g, -1).wait_recv()
            to_core(g).start()
            return
        for k in (1, 3, 2):
            ag(g, stage, k).wait_recv()
        ag_start(g, stage - 1)
        for k in (1, 2, 3):
            if stage == 2:
                rs(g, 2, k).wait_send()
            else:
                ag(g, 2, k).wait_send()

    tacc[...] = jnp.zeros_like(tacc)

    def backward(i, _):
        @pl.when(i >= EARLY)
        def _():
            forward_cot(i)

        s = at(i * CC, CC)
        cot_z(i, c4).wait_recv()
        da = nt(cotv[s], tw[0]) + m1 * nt(c2[s], tw[1]) + m2 * nt(c4[s], tw[2])
        dp = (da.astype(BF16).astype(F32) * slope[s]).astype(BF16)
        e = at(WID + i * CC, CC)
        d[1, e] = dp
        dp = dp.astype(F32)
        d[0, e] = left_by_one(dp, CC)
        d[2, e] = right_by_one(dp, CC)
        tacc[0] += tn(a0[s], c2[s])
        tacc[1] += tn(a0[s], c4[s])
        return 0

    lax.fori_loop(0, 1, backward, 0)
    open_group(0)
    lax.fori_loop(1, 3, backward, 0)
    close_stage(0, 0)
    lax.fori_loop(3, 4, backward, 0)
    close_stage(0, 1)
    lax.fori_loop(4, 5, backward, 0)
    close_stage(0, 2)
    lax.fori_loop(5, 6, backward, 0)
    ag_close(0, 2)
    lax.fori_loop(6, 7, backward, 0)
    ag_close(0, 1)
    lax.fori_loop(7, NCOT, backward, 0)
    ag_pass(0)

    def act_z(src, r):
        s = at(r * FC, FC)
        return remote(src.at[s], a2.at[s], az_s.at[r], az_r.at[r], zpair)

    emit(1, m1 * tacc[0])
    emit(2, m2 * tacc[1])

    def spatial_tap(t):
        i, j = divmod(t - 3, 3)
        emit(t, tn(v[1, pl.ds(WID, HW)], d[j, pl.ds((2 - i) * WID, HW)]))

    def grad_video(r, _):
        acc = None
        for i in range(3):
            for j in range(3):
                t = nt(d[j, at(r * FC + (2 - i) * WID, FC)], w[3 * i + j])
                acc = t if acc is None else acc + t
        s = at(r * FC, FC)
        gvv[s] = (cotv[s].astype(F32) + acc).astype(BF16)
        return 0

    def mix(r, _):
        s = at(r * FC, FC)
        t = nn(a0[s], tw[0]) + k1 * nn(a2[s], tw[1]) + k2 * nn(a4[s], tw[2])
        t = t.astype(BF16).astype(F32)
        outv[s] = (v[1, at(WID + r * FC, FC)].astype(F32) + t).astype(BF16)
        return 0

    def forward_act(r):
        act_y(r).wait_recv()

        @pl.when(low)
        def _():
            act_z(a0, r).start()

        @pl.when(jnp.logical_not(low))
        def _():
            act_z(a4, r).start()

    def drain_cot(i, _):
        cot_y(i).wait_send()
        cot_z(i, c4).wait_send()
        return 0

    def drain_core(t, _):
        core_half(t).wait_send()
        return 0

    def drain_act(r, _):
        act_y(r).wait_send()
        act_z(a0, r).wait_send()
        return 0

    def act_here(r, _):
        act_z(a0, r).wait_recv()
        return 0

    def mix_all():
        lax.fori_loop(0, NFWD, act_here, 0)
        lax.fori_loop(0, NFWD, mix, 0)
        lax.fori_loop(0, NFWD, drain_act, 0)

    forward_act(0)
    forward_act(1)
    spatial_tap(3)
    open_group(1)
    forward_act(2)
    spatial_tap(4)
    spatial_tap(5)
    open_group(2)
    spatial_tap(6)
    spatial_tap(7)
    open_group(3)
    spatial_tap(8)
    spatial_tap(9)
    open_group(4)
    forward_act(3)
    spatial_tap(10)
    open_group(5)
    spatial_tap(11)
    lax.fori_loop(0, 1, grad_video, 0)
    open_group(6)

    steps = []
    for g in range(1, NG):
        for n, after in enumerate(AFTER):
            steps.append((OPENED[g] + after, g, n))
    for n in range(1, 4):
        steps.append((GRAD_VIDEO_AT[n], 0, 10 + n))
    steps.append((MIX_AT, 0, 20))
    steps.append((45.1, 0, 6))
    for _, g, n in sorted(steps):
        if n == 20:
            mix_all()
        elif n >= 10:
            lax.fori_loop(n - 10, n - 9, grad_video, 0)
            if n == 11:
                lax.fori_loop(0, NCOT, drain_cot, 0)
            if n == 12:
                lax.fori_loop(0, TAPS, drain_core, 0)
        elif n < 3:
            close_stage(g, n)
        elif n < 5:
            ag_close(g, 5 - n)
        elif n == 5:
            ag_pass(g)
        else:
            ag_close(g, 0)
    for g in range(NG):
        to_core(g).wait_recv()
        for k in (1, 3):
            ag(g, 0, k).wait_send()
        passed(g, 1).wait_send()
        passed(g, -1).wait_send()
        to_core(g).wait_send()


def finish(scale, grads, out_in, gv_in, spatial, temporal, out, gv, held, sem):
    copies = [
        pltpu.make_async_copy(out_in, out, sem.at[TAPS]),
        pltpu.make_async_copy(gv_in, gv, sem.at[TAPS + 1]),
    ]
    for c in copies:
        c.start()
    for t in range(TAPS):
        for b in range(4):
            held[t, :, b * 128 : (b + 1) * 128] = grads[t, b].astype(F32) * scale
        to = temporal.at[t] if t < 3 else spatial.at[t - 3]
        copies.append(pltpu.make_async_copy(held.at[t], to, sem.at[t]))
        copies[-1].start()
    for c in copies:
        c.wait()


def on_device(video, w_spatial, temporal_weight, clip_frame_counts, cotangent):
    dma = pltpu.SemaphoreType.DMA
    any_spec = pl.BlockSpec(memory_space=pl.ANY)
    vmem_spec = pl.BlockSpec(memory_space=pltpu.VMEM)
    frame = (HW, C)
    out, gv, grads = pl.pallas_call(
        kernel,
        out_shape=(
            pltpu.VMEM(frame, BF16),
            pltpu.VMEM(frame, BF16),
            pltpu.VMEM((TAPS, 4, C, 128), BF16),
        ),
        in_specs=[any_spec, any_spec, any_spec, pl.BlockSpec(memory_space=pltpu.SMEM), any_spec],
        out_specs=(vmem_spec, vmem_spec, vmem_spec),
        scratch_shapes=[
            pltpu.VMEM((3, PAD, C), BF16),
            pltpu.VMEM((3, PAD, C), BF16),
            pltpu.VMEM(frame, BF16),
            pltpu.VMEM(frame, BF16),
            pltpu.VMEM(frame, BF16),
            pltpu.VMEM(frame, BF16),
            pltpu.VMEM(frame, BF16),
            pltpu.VMEM(frame, BF16),
            pltpu.VMEM(frame, F32),
            pltpu.VMEM((9, C, C), BF16),
            pltpu.VMEM((3, C, C), BF16),
            pltpu.VMEM((2, C, C), F32),
            pltpu.VMEM((TAPS, 4, C, 128), BF16),
            pltpu.VMEM((TAPS, 4, 256, 128), BF16),
            pltpu.VMEM((TAPS, 4, 256, 128), BF16),
            pltpu.VMEM((3, TAPS, 256, 128), BF16),
            pltpu.VMEM((TAPS, 256, 128), BF16),
            pltpu.VMEM((3, TAPS, 64, 128), BF16),
            pltpu.VMEM((TAPS, 64, 128), BF16),
            pltpu.VMEM((3, TAPS, 16, 128), BF16),
            dma((4,)),
            dma((NCOT,)), dma((NCOT,)), dma((NCOT,)), dma((NCOT,)),
            dma((NFWD,)), dma((NFWD,)), dma((NFWD,)), dma((NFWD,)),
            dma((TAPS,)), dma((TAPS,)),
            dma((NG, 3, 3)), dma((NG, 3, 3)), dma((NG, 3, 3)), dma((NG, 3, 3)),
            dma((NG, 2)), dma((NG, 2)), dma((NG,)), dma((NG,)),
        ],
        compiler_params=pltpu.CompilerParams(
            collective_id=0, has_side_effects=True, vmem_limit_bytes=54 << 20
        ),
        name="block",
    )(
        video.reshape(frame),
        w_spatial.reshape(9, C, C),
        temporal_weight,
        clip_frame_counts,
        cotangent.reshape(frame),
    )
    scale = 1.0 / float(FRAMES * HW) ** 0.5
    spatial, temporal, out, gv = pl.pallas_call(
        functools.partial(finish, scale),
        out_shape=(
            jax.ShapeDtypeStruct((9, C, C), F32),
            jax.ShapeDtypeStruct((3, C, C), F32),
            jax.ShapeDtypeStruct(frame, BF16),
            jax.ShapeDtypeStruct(frame, BF16),
        ),
        in_specs=[vmem_spec, vmem_spec, vmem_spec],
        out_specs=(any_spec, any_spec, any_spec, any_spec),
        scratch_shapes=[pltpu.VMEM((TAPS, C, C), F32), dma((TAPS + 2,))],
        compiler_params=pltpu.CompilerParams(vmem_limit_bytes=24 << 20),
        name="finish",
    )(*(pltpu.with_memory_space_constraint(a, pltpu.VMEM) for a in (grads, out, gv)))
    return (
        out.reshape(video.shape),
        gv.reshape(video.shape),
        spatial.reshape(3, 3, C, C),
        temporal,
    )


def solution(mesh):
    frames = P(("frame", "row"), None, None, None)
    return jax.shard_map(
        on_device,
        mesh=mesh,
        in_specs=(frames, P(), P(), P(), frames),
        out_specs=(frames, frames, P(), P()),
        check_vma=False,
    )
```
